32 devices in a mesh: group: 2 (over y), ctx: 8 (over z, x), tp: 2 (over core).
Axes of the slice: x: 2, y: 2, z: 4, core: 2. Of those that a mesh axis runs over, the one named last changes fastest.
Arguments:
- hidden: bfloat16 [256, 16384], P(('group', 'ctx')), parts along dimension 0, may hold values from -6 to 6
- q_base: bfloat16 [256, 8192], P(('group', 'ctx'), 'tp'), parts along dimension 0, may hold values from -6 to 6
- adapter_down: bfloat16 [16, 16384, 64], P(('group', 'ctx')), parts along dimension 0, may hold values from -0.046875 to 0.046875
- adapter_up: bfloat16 [16, 64, 8192], P(('group', 'ctx'), None, 'tp'), parts along dimension 0, may hold values from -0.75 to 0.75
- adapter_owner: int32 [2], P('group'), parts along dimension 0, may hold values from 0 to 7
- turn_start: int32 [2], P('group'), parts along dimension 0, may hold values from 512 to 2047
- shard_lengths: int32 [16], P('group'), parts along dimension 0, may hold values from 1 to 64, 384 in all
- stored_keys: bfloat16 [1024, 512], P(('group', 'ctx'), 'tp'), parts along dimension 0, may hold values from -250 to 250
- stored_values: bfloat16 [1024, 512], P(('group', 'ctx'), 'tp'), parts along dimension 0, may hold values from -6 to 6
- unrotated_turn_keys: bfloat16 [256, 512], P(('group', 'ctx'), 'tp'), parts along dimension 0, may hold values from -15 to 15
- incoming_values: bfloat16 [256, 512], P(('group', 'ctx'), 'tp'), parts along dimension 0, may hold values from -6 to 6
Outputs:
- attended: bfloat16 [256, 8192], P(('group', 'ctx'), 'tp'), parts along dimension 0
The draws below stay inside these ranges and needn't reach their ends.
There are 2 independent parts, one for each index of `group`. The reference program is written for one: setup_inputs(seed, part) draws one part's arguments, and reference() takes and returns one part's arrays. A program takes and returns all parts, laid end to end along the dimension named above; each array names one. Nothing has to cross between parts.
Inputs may be any that keep to these rules, and one draw needn't show every extreme that they name: The used slots of shard s are its slots 0 .. shard_lengths[s] - 1; some shard uses all 64.
All inputs are finite; a program needn't handle non-finite values.
Results may differ from the reference program's by a relative error of at most 0.019.
The reference program's roundings to bfloat16 on the way count: a program that leaves them out, or rounds other values in their place, can miss the bound.
Values may be sent and summed in bfloat16 or wider, within the bound.
No kernel may reach another device: no remote copies, remote signals or barrier semaphores. Data moves between devices by JAX's collectives and lax.ppermute only.
A program may use at most 64 MiB of HBM per device.

```python
import math
import jax
import jax.numpy as jnp
import numpy as np
from jax import lax

D = 16384
QUERY_HEAD_COUNT = 64
KEY_VALUE_HEADS = 4
HEAD_SIZE = 128
RANK = 64
QUERY_PER_SHARD = 16
CACHE_PER_SHARD = 64
TURN_TOKENS = 128
CACHE_SLOTS_ALL = 512
N_CTX = 8


def draw_stored_keys(key, part):
    leading_key = jax.random.fold_in(jax.random.fold_in(key, 71), 0)
    drawn = jnp.clip(jax.random.normal(leading_key, (CACHE_SLOTS_ALL, KEY_VALUE_HEADS * HEAD_SIZE), jnp.float32) * 2.5, -15.0, 15.0)
    return drawn.astype(jnp.bfloat16)


def level_of(own_key, shape, shards, least, top_value):
    level, own = 1.0, jax.random.fold_in(own_key, 6)
    for axis_at, shards_of in shards:
        heights = jnp.exp(jax.random.uniform(jax.random.fold_in(own, axis_at), (shards_of,), jnp.float32, least / len(shards), top_value / len(shards)))
        level = level * jnp.repeat(heights, shape[axis_at] // shards_of).reshape([-1 if axis == axis_at else 1 for axis in range(len(shape))])
    return level


def split_up(number_of, total, most, lean):
    loads = [(1 << 20) // math.isqrt(grade ** lean) + 1 for grade in range(2, number_of + 1)]
    surplus, holding = total - most - (number_of - 1), [1] * (number_of - 1)
    while surplus > 0:
        free = [i for i in range(number_of - 1) if holding[i] < most]
        mass, remaining = sum([loads[i] for i in free]), surplus
        for i in free:
            extra = min(most - holding[i], max(1, remaining * loads[i] // mass), surplus)
            holding[i] = holding[i] + extra
            surplus = surplus - extra
    return np.array([most] + holding)


def ragged_sizes(key, count, total, limit, skew):
    if count == 2:
        one = jax.random.randint(key, (), max(1, total - limit), min(limit, total - 1) + 1)
        return jnp.stack([one, total - one])
    sizes = jnp.asarray(split_up(count, total, limit, skew), jnp.int32)
    twos = (count - 1) // 2
    donor, taker = sizes[1:1 + 2 * twos:2], sizes[2:2 + 2 * twos:2]
    room = jnp.minimum(donor - 1, limit - taker)
    moved = jax.random.randint(jax.random.fold_in(key, 1), (twos,), 0, 1 << 20) % (room + 1)
    sizes = sizes.at[1:1 + 2 * twos:2].set(donor - moved).at[2:2 + 2 * twos:2].set(taker + moved)
    return sizes[jax.random.permutation(jax.random.fold_in(key, 2), count)]


def gaussian(key, extent, width, most, cuts=(), kind=jnp.bfloat16):
    values = jax.random.normal(key, extent, jnp.float32) * width
    if len(cuts) > 0:
        values = level_of(key, extent, cuts, -0.22, 0.18) * values
    return jnp.clip(values, min=-most, max=most).astype(kind)


def setup_inputs(seed: int = 0, part: int = 0) -> dict:
    streams_of = jax.random.split(jax.random.key(seed), 12)
    part_keys = jax.random.split(jax.random.fold_in(streams_of[11], part), 12)
    return {
        "hidden": gaussian(part_keys[0], (TURN_TOKENS, D), 1.0, 6.0, ((0, 8),)),
        "q_base": gaussian(part_keys[1], (TURN_TOKENS, QUERY_HEAD_COUNT * HEAD_SIZE), 1.0, 6.0, ((0, 8), (1, 2))),
        "adapter_down": gaussian(part_keys[2], (N_CTX, D, RANK), D ** -0.5, 0.046875, ((0, 8),)),
        "adapter_up": gaussian(part_keys[3], (N_CTX, RANK, QUERY_HEAD_COUNT * HEAD_SIZE), RANK ** -0.5, 0.75, ((0, 8), (2, 2))),
        "adapter_owner": jax.random.randint(part_keys[4], (1,), 0, N_CTX).astype(jnp.int32),
        "turn_start": jax.random.randint(part_keys[5], (1,), CACHE_SLOTS_ALL, 4 * CACHE_SLOTS_ALL).astype(jnp.int32),
        "shard_lengths": ragged_sizes(part_keys[6], N_CTX, N_CTX * CACHE_PER_SHARD * 3 // 4, CACHE_PER_SHARD, 1).astype(jnp.int32),
        "stored_keys": draw_stored_keys(jax.random.fold_in(jax.random.fold_in(streams_of[11], part), 71), part),
        "stored_values": gaussian(part_keys[8], (CACHE_SLOTS_ALL, KEY_VALUE_HEADS * HEAD_SIZE), 1.0, 6.0, ((0, 8), (1, 2))),
        "unrotated_turn_keys": gaussian(part_keys[9], (TURN_TOKENS, KEY_VALUE_HEADS * HEAD_SIZE), 2.5, 15.0, ((0, 8), (1, 2))),
        "incoming_values": gaussian(part_keys[10], (TURN_TOKENS, KEY_VALUE_HEADS * HEAD_SIZE), 1.0, 6.0, ((0, 8), (1, 2))),
    }


def apply_rotary(values, token_positions, heads):
    half_dim = HEAD_SIZE // 2
    inverse = jnp.exp(jnp.arange(half_dim, dtype=jnp.float32) * (-2.0 * math.log(500000.0) / HEAD_SIZE))
    angles = token_positions.astype(jnp.float32)[:, None] * inverse[None, :]
    cosine = jnp.cos(angles)[:, None, :]
    sine = jnp.sin(angles)[:, None, :]
    shaped = values.reshape(values.shape[0], heads, HEAD_SIZE)
    first = shaped[..., :half_dim]
    second = shaped[..., half_dim:]
    turned = jnp.concatenate([first * cosine - second * sine, second * cosine + first * sine], axis=-1)
    return turned.reshape(values.shape[0], heads * HEAD_SIZE)

def reference(hidden, q_base, adapter_down, adapter_up, adapter_owner, turn_start, shard_lengths, stored_keys, stored_values, unrotated_turn_keys, incoming_values):
    adapter_a = adapter_down[adapter_owner[0]]
    adapter_b = adapter_up[adapter_owner[0]]
    lowrank = jnp.dot(hidden, adapter_a, preferred_element_type=jnp.float32).astype(jnp.bfloat16)
    adapter_delta = jnp.dot(lowrank, adapter_b, preferred_element_type=jnp.float32)
    token_positions = turn_start[0] + jnp.arange(TURN_TOKENS, dtype=jnp.int32)
    query_rows = apply_rotary(q_base.astype(jnp.float32) + 0.5 * adapter_delta, token_positions, QUERY_HEAD_COUNT).astype(jnp.bfloat16)
    rotated_turn_keys = apply_rotary(unrotated_turn_keys.astype(jnp.float32), token_positions, KEY_VALUE_HEADS).astype(jnp.bfloat16)
    key_head_rows = jnp.concatenate([stored_keys, rotated_turn_keys], axis=0).astype(jnp.float32).reshape(-1, KEY_VALUE_HEADS, HEAD_SIZE)
    value_head_rows = jnp.concatenate([stored_values, incoming_values], axis=0).astype(jnp.float32).reshape(-1, KEY_VALUE_HEADS, HEAD_SIZE)
    slot_index = jnp.arange(CACHE_SLOTS_ALL, dtype=jnp.int32)
    cache_used = slot_index % CACHE_PER_SHARD < shard_lengths[slot_index // CACHE_PER_SHARD]
    turn_index = jnp.arange(TURN_TOKENS, dtype=jnp.int32)
    score_scale = 1.0 / math.sqrt(HEAD_SIZE)
    block_list = query_rows.astype(jnp.float32).reshape(TURN_TOKENS // QUERY_PER_SHARD, QUERY_PER_SHARD, KEY_VALUE_HEADS, QUERY_HEAD_COUNT // KEY_VALUE_HEADS, HEAD_SIZE)
    firsts = jnp.arange(TURN_TOKENS // QUERY_PER_SHARD, dtype=jnp.int32) * QUERY_PER_SHARD

    def one_block(inputs):
        block, first = inputs
        scores = jnp.einsum('rhgd,khd->rhgk', block, key_head_rows) * score_scale
        mine = first + jnp.arange(QUERY_PER_SHARD, dtype=jnp.int32)
        turn_used = turn_index[None, :] <= mine[:, None]
        allowed = jnp.concatenate([jnp.broadcast_to(cache_used[None, :], (QUERY_PER_SHARD, CACHE_SLOTS_ALL)), turn_used], axis=1)
        allowed = allowed[:, None, None, :]
        highest = lax.optimization_barrier(jnp.max(jnp.where(allowed, scores, -1e+30), axis=-1))
        weights = jnp.where(allowed, jnp.exp(scores - highest[..., None]), 0.0)
        denominator = lax.optimization_barrier(jnp.sum(weights, axis=-1))
        rounded = lax.optimization_barrier(weights.astype(jnp.bfloat16)).astype(jnp.float32)
        numerator = jnp.einsum('rhgk,khd->rhgd', rounded, value_head_rows)
        return numerator / denominator[..., None]
    result = lax.map(one_block, (block_list, firsts))
    return result.reshape(TURN_TOKENS, QUERY_HEAD_COUNT * HEAD_SIZE).astype(jnp.bfloat16)
```

```python
import functools
import math

import jax
import jax.numpy as jnp
from jax import lax
from jax.experimental import pallas as pl
from jax.experimental.pallas import tpu as pltpu
from jax.sharding import PartitionSpec as P

HEAD_SIZE = 128
LANES = 128


def rotary_tables(token_positions):
    half_dim = HEAD_SIZE // 2
    inverse = jnp.exp(
        jnp.arange(half_dim, dtype=jnp.float32) * (-2.0 * math.log(500000.0) / HEAD_SIZE)
    )
    angles = token_positions.astype(jnp.float32)[:, None] * inverse[None, :]
    return jnp.cos(angles), jnp.sin(angles)


def spread(shard, axis, root):
    mine = lax.axis_index(axis) == root
    return lax.psum(jnp.where(mine, shard, jnp.zeros_like(shard)), axis)


def apply_rotary(values, token_positions, heads):
    half_dim = HEAD_SIZE // 2
    cosine, sine = rotary_tables(token_positions)
    cosine, sine = cosine[:, None, :], sine[:, None, :]
    shaped = values.reshape(values.shape[0], heads, HEAD_SIZE)
    first = shaped[..., :half_dim]
    second = shaped[..., half_dim:]
    turned = jnp.concatenate(
        [first * cosine - second * sine, second * cosine + first * sine], axis=-1
    )
    return turned.reshape(values.shape[0], heads * HEAD_SIZE)


def shards_any(
    hidden,
    q_base,
    adapter_down,
    adapter_up,
    adapter_owner,
    turn_start,
    shard_lengths,
    stored_keys,
    stored_values,
    unrotated_turn_keys,
    incoming_values,
):
    holder = adapter_owner[0]
    got_down, got_up = (
        spread(adapter_down[0], "ctx", holder),
        spread(adapter_up[0], "ctx", holder),
    )
    lowrank = jnp.dot(hidden, got_down, preferred_element_type=jnp.float32).astype(jnp.bfloat16)
    adapter_delta = jnp.dot(lowrank, got_up, preferred_element_type=jnp.float32)
    token_count = q_base.shape[0]
    slot_count = stored_keys.shape[0]
    shard_rows = token_count + slot_count
    ctx_size = lax.axis_size("ctx")
    myself = lax.axis_index("ctx")
    query_heads = q_base.shape[1] // HEAD_SIZE
    kv_heads = unrotated_turn_keys.shape[1] // HEAD_SIZE
    groups = query_heads // kv_heads
    local_tokens = jnp.arange(token_count, dtype=jnp.int32)
    token_positions = turn_start[0] + myself * token_count + local_tokens
    query_rows = apply_rotary(
        q_base.astype(jnp.float32) + 0.5 * adapter_delta, token_positions, query_heads
    ).astype(jnp.bfloat16)
    rotated_turn_keys = apply_rotary(
        unrotated_turn_keys.astype(jnp.float32), token_positions, kv_heads
    ).astype(jnp.bfloat16)
    grouped = query_rows.reshape(token_count, kv_heads, groups, HEAD_SIZE)
    key_here = jnp.concatenate([stored_keys, rotated_turn_keys], axis=0)
    value_here = jnp.concatenate([stored_values, incoming_values], axis=0)
    mine = myself * token_count + local_tokens
    score_scale = 1.0 / math.sqrt(HEAD_SIZE)
    shard_ids = jnp.arange(ctx_size, dtype=jnp.int32)

    def absorb(state, key_block, value_block, start):
        highest, denominator, accum = state
        row_count = key_block.shape[0]
        global_rows = start + jnp.arange(row_count, dtype=jnp.int32)
        owner_shard = global_rows // shard_rows
        within = global_rows % shard_rows
        is_cache = within < slot_count
        lengths_here = jnp.sum(
            jnp.where(owner_shard[:, None] == shard_ids[None, :], shard_lengths[None, :], 0), axis=1
        )
        token_number = owner_shard * token_count + (within - slot_count)
        allowed = jnp.where(
            is_cache[None, :],
            (within < lengths_here)[None, :],
            token_number[None, :] <= mine[:, None],
        )
        allowed = allowed[:, None, None, :]
        key_head_rows = key_block.reshape(-1, kv_heads, HEAD_SIZE)
        value_head_rows = value_block.reshape(-1, kv_heads, HEAD_SIZE)
        scores = (
            jnp.einsum("rhgd,khd->rhgk", grouped, key_head_rows, preferred_element_type=jnp.float32)
            * score_scale
        )
        new_high = jnp.maximum(highest, jnp.max(jnp.where(allowed, scores, -1e30), axis=-1))
        weights = jnp.where(allowed, jnp.exp(scores - new_high[..., None]), 0.0)
        fade = jnp.exp(highest - new_high)
        denominator = denominator * fade + jnp.sum(weights, axis=-1)
        product = jnp.einsum(
            "rhgk,khd->rhgd",
            weights.astype(jnp.bfloat16),
            value_head_rows,
            preferred_element_type=jnp.float32,
        )
        accum = accum * fade[..., None] + product
        return (new_high, denominator, accum)

    state = (
        jnp.full((token_count, kv_heads, groups), -1e30, jnp.float32),
        jnp.zeros((token_count, kv_heads, groups), jnp.float32),
        jnp.zeros((token_count, kv_heads, groups, HEAD_SIZE), jnp.float32),
    )
    block_rows = shard_rows * 8
    keys = lax.all_gather(key_here, "ctx", axis=0, tiled=True)
    values = lax.all_gather(value_here, "ctx", axis=0, tiled=True)
    row_count = keys.shape[0]
    if row_count > block_rows and row_count % block_rows == 0:
        count = row_count // block_rows
        key_split = keys.reshape(count, block_rows, keys.shape[1])
        value_split = values.reshape(count, block_rows, values.shape[1])

        def inner(carry, items):
            key_one, value_one, number = items
            return (absorb(carry, key_one, value_one, number * block_rows), None)

        numbers = jnp.arange(count, dtype=jnp.int32)
        state, unused = lax.scan(inner, state, (key_split, value_split, numbers))
    else:
        state = absorb(state, keys, values, jnp.int32(0))
    highest, denominator, accum = state
    attended = accum / denominator[..., None]
    return attended.reshape(token_count, query_heads * HEAD_SIZE).astype(jnp.bfloat16)


def pack_kernel(cos_ref, sin_ref, sk_ref, sv_ref, tk_ref, tv_ref, kv_ref):
    slots, width = sk_ref.shape
    tokens = tk_ref.shape[0]
    rows = slots + tokens
    kv_ref[0:slots, :] = sk_ref[...]
    kv_ref[rows : rows + slots, :] = sv_ref[...]
    kv_ref[rows + slots : 2 * rows, :] = tv_ref[...]
    cosine, sine = cos_ref[...], sin_ref[...]
    for h in range(width // HEAD_SIZE):
        at = slice(h * HEAD_SIZE, (h + 1) * HEAD_SIZE)
        v = tk_ref[:, at].astype(jnp.float32)
        turned = v * cosine + pltpu.roll(v, HEAD_SIZE // 2, 1) * sine
        kv_ref[slots:rows, at] = turned.astype(kv_ref.dtype)


def partial_kernel(z_size, x_size, chunks, pick_ref, *refs):
    pos = 0
    near = refs[pos : pos + z_size]
    pos += z_size
    far = refs[pos : pos + x_size - 1]
    pos += x_size - 1
    shares = [refs[pos + c * z_size : pos + (c + 1) * z_size] for c in range(chunks)]
    pos += chunks * z_size
    out_ref, a_ref = refs[pos], refs[pos + 1]
    pick = pick_ref[0]
    rank = a_ref.shape[0]
    step = rank // chunks
    for c in range(chunks):
        for s in range(z_size):

            @pl.when(pick == s)
            def _(c=c, s=s):
                a_ref[c * step : (c + 1) * step, :] = shares[c][s][...]

    a = a_ref[...]
    for f in range(x_size):
        for s in range(z_size):
            h = near[s][0] if f == 0 else far[f - 1][s]
            out_ref[f, s] = lax.dot_general(
                h, a, (((1,), (1,)), ((), ())), preferred_element_type=jnp.float32
            )


def attend_kernel(z_size, x_size, slots, meta_ref, len_ref, *refs):
    n = z_size * x_size
    low = refs[0:z_size]
    ups = refs[z_size : z_size + n]
    kvs = refs[z_size + n : z_size + 2 * n]
    cos_ref, sin_ref, q_ref, o_ref, d_ref, qs_ref, k_ref, v_ref = refs[z_size + 2 * n :]
    tokens = q_ref.shape[0]
    rows = kvs[0].shape[0] // 2
    width = d_ref.shape[2]
    query_heads = q_ref.shape[1] // HEAD_SIZE
    kv_heads = k_ref.shape[1] // HEAD_SIZE
    groups = query_heads // kv_heads
    myself = meta_ref[n]
    total = low[0][...]
    for r in low[1:]:
        total = total + r[...]
    lowrank = total.astype(jnp.bfloat16)
    for i in range(n):
        d_ref[meta_ref[i]] = jnp.dot(lowrank, ups[i][...], preferred_element_type=jnp.float32)
    for i in range(n):
        k_ref[i * rows : (i + 1) * rows, :] = kvs[i][0:rows, :]
        v_ref[i * rows : (i + 1) * rows, :] = kvs[i][rows : 2 * rows, :]
    cosine, sine = cos_ref[...], sin_ref[...]
    for h in range(query_heads):
        b, off = divmod(h * HEAD_SIZE, width)
        v = q_ref[:, h * HEAD_SIZE : (h + 1) * HEAD_SIZE].astype(jnp.float32)
        v = v + 0.5 * d_ref[b, :, off : off + HEAD_SIZE]
        turned = v * cosine + pltpu.roll(v, HEAD_SIZE // 2, 1) * sine
        g = h % groups
        qs_ref[h // groups, g * tokens : (g + 1) * tokens, :] = turned.astype(jnp.bfloat16)
    shape = (tokens, n * rows)
    col = lax.broadcasted_iota(jnp.int32, shape, 1)
    token = myself * tokens + lax.broadcasted_iota(jnp.int32, shape, 0)
    start = jnp.zeros(shape, jnp.int32)
    limit = jnp.zeros(shape, jnp.int32)
    first = jnp.zeros(shape, jnp.int32)
    for i in range(n):
        after = col >= i * rows
        start = jnp.where(after, i * rows, start)
        limit = jnp.where(after, len_ref[i], limit)
        first = jnp.where(after, meta_ref[n + 1 + i] * tokens, first)
    within = col - start
    ok = jnp.where(within < slots, within - limit, within - slots + first - token - 1) < 0
    bias = jnp.where(ok, 0.0, -1e30)[None]
    scale = 1.0 / math.sqrt(HEAD_SIZE)
    for kv in range(kv_heads):
        at = slice(kv * HEAD_SIZE, (kv + 1) * HEAD_SIZE)
        s = lax.dot_general(
            qs_ref[kv], k_ref[:, at], (((1,), (1,)), ((), ())), preferred_element_type=jnp.float32
        )
        s = s.reshape(groups, tokens, n * rows) * scale + bias
        w = jnp.exp(s - jnp.max(s, axis=-1, keepdims=True))
        denominator = jnp.sum(w, axis=-1, keepdims=True)
        w = w.reshape(groups * tokens, n * rows).astype(jnp.bfloat16)
        o = jnp.dot(w, v_ref[:, at], preferred_element_type=jnp.float32)
        o = o.reshape(groups, tokens, HEAD_SIZE) / denominator
        for g in range(groups):
            h = kv * groups + g
            o_ref[:, h * HEAD_SIZE : (h + 1) * HEAD_SIZE] = o[g].astype(o_ref.dtype)


def vmem(count):
    return [pl.BlockSpec(memory_space=pltpu.VMEM)] * count


def smem(count):
    return [pl.BlockSpec(memory_space=pltpu.SMEM)] * count


def shards_two_level(
    x_size,
    chunks,
    hidden,
    q_base,
    adapter_down,
    adapter_up,
    adapter_owner,
    turn_start,
    shard_lengths,
    stored_keys,
    stored_values,
    unrotated_turn_keys,
    incoming_values,
):
    n = lax.axis_size("ctx")
    tp_size = lax.axis_size("tp")
    z_size = n // x_size
    myself = lax.axis_index("ctx")
    core = lax.axis_index("tp")
    z, x = myself // x_size, myself % x_size
    owner = adapter_owner[0]
    owner_z, owner_x = owner // x_size, owner % x_size
    tokens, features = hidden.shape
    share = features // (tp_size * n)
    rank = adapter_down.shape[2]
    step = rank // chunks
    columns = adapter_up.shape[2]
    width = columns // n
    slots = stored_keys.shape[0]

    def along_z(v, s):
        pairs = [
            (a * x_size + b, (a + s) % z_size * x_size + b)
            for a in range(z_size)
            for b in range(x_size)
        ]
        return lax.ppermute(v, "ctx", pairs)

    def along_x(v, f, g=0):
        pairs = [
            (
                (a * x_size + b) * tp_size + c,
                (a * x_size + (b + f) % x_size) * tp_size + (c + g) % tp_size,
            )
            for a in range(z_size)
            for b in range(x_size)
            for c in range(tp_size)
        ]
        return lax.ppermute(v, ("ctx", "tp"), pairs)

    def choose(which, options):
        out = options[0]
        for i, option in enumerate(options[1:], 1):
            out = jnp.where(which == i, option, out)
        return out

    cut = lax.dynamic_slice_in_dim
    from_x = (x - owner_x) % x_size
    from_z = (z - owner_z) % z_size

    down = adapter_down[0].T
    shares = []
    for c in range(chunks):
        rows = down[c * step : (c + 1) * step]

        def part(xt, rows=rows):
            return cut(rows, (core * x_size + xt) * z_size * share, z_size * share, 1)

        got = [part(x)] + [
            along_x(part((x + f) % x_size), f) for f in range(1, x_size)
        ]
        row_part = choose(from_x, got)
        shares += [cut(row_part, z * share, share, 1)] + [
            along_z(cut(row_part, (z + s) % z_size * share, share, 1), s) for s in range(1, z_size)
        ]

    def own(xt, zt):
        return cut(hidden, ((core * x_size + xt) * z_size + zt) * share, share, 1)

    near = []
    for s in range(z_size):
        piece = jnp.stack([own((x + f) % x_size, (z + s) % z_size) for f in range(x_size)])
        near.append(along_z(piece, s) if s else piece)
    far = [along_x(jnp.stack([p[f] for p in near]), f) for f in range(1, x_size)]

    up = adapter_up[0]
    got = [cut(up, x * z_size * width, z_size * width, 1)] + [
        along_x(cut(up, (x + f) % x_size * z_size * width, z_size * width, 1), f)
        for f in range(1, x_size)
    ]
    row_part = choose(from_x, got)
    mine = choose(
        from_z,
        [cut(row_part, z * width, width, 1)]
        + [along_z(cut(row_part, (z + s) % z_size * width, width, 1), s) for s in range(1, z_size)],
    )
    ups = [mine] + [along_z(mine, s) for s in range(1, z_size)]
    ups += [along_x(u, f) for f in range(1, x_size) for u in ups[:z_size]]

    positions = turn_start[0] + myself * tokens + jnp.arange(tokens, dtype=jnp.int32)
    cosine, sine = rotary_tables(positions)
    cosine = jnp.concatenate([cosine, cosine], axis=1)
    sine = jnp.concatenate([-sine, sine], axis=1)
    kv_rows = 2 * (slots + tokens)
    kv = pl.pallas_call(
        pack_kernel,
        out_shape=jax.ShapeDtypeStruct((kv_rows, stored_keys.shape[1]), jnp.bfloat16),
        in_specs=vmem(6),
        out_specs=vmem(1)[0],
        name="pack",
    )(cosine, sine, stored_keys, stored_values, unrotated_turn_keys, incoming_values)
    kvs = [kv] + [along_z(kv, s) for s in range(1, z_size)]
    kvs += [along_x(v, f) for f in range(1, x_size) for v in kvs[:z_size]]

    partial = pl.pallas_call(
        functools.partial(partial_kernel, z_size, x_size, chunks),
        out_shape=jax.ShapeDtypeStruct((x_size, z_size, tokens, rank), jnp.float32),
        in_specs=smem(1) + vmem(z_size + x_size - 1 + chunks * z_size),
        out_specs=vmem(1)[0],
        scratch_shapes=[pltpu.VMEM((rank, share), jnp.bfloat16)],
        name="lowrank",
    )(from_z.reshape(1), *near, *far, *shares)
    summed = partial[0]
    for f in range(x_size):
        for g in range(tp_size):
            if f or g:
                summed = summed + along_x(partial[f], -f, g)
    low = [summed[0]] + [along_z(summed[s], -s) for s in range(1, z_size)]

    offsets = [(s, f) for f in range(x_size) for s in range(z_size)]
    sources = [((z - s) % z_size, (x - f) % x_size) for s, f in offsets]
    blocks = [b * z_size + a for a, b in sources]
    ids = [a * x_size + b for a, b in sources]
    meta = jnp.stack(blocks + [myself] + ids)
    lengths = shard_lengths[jnp.stack(ids)]
    kv_width = stored_keys.shape[1]
    return pl.pallas_call(
        functools.partial(attend_kernel, z_size, x_size, slots),
        out_shape=jax.ShapeDtypeStruct(q_base.shape, jnp.bfloat16),
        in_specs=smem(2) + vmem(z_size + 2 * n + 3),
        out_specs=vmem(1)[0],
        scratch_shapes=[
            pltpu.VMEM((n, tokens, width), jnp.float32),
            pltpu.VMEM(
                (kv_width // HEAD_SIZE, columns // kv_width * tokens, HEAD_SIZE), jnp.bfloat16
            ),
            pltpu.VMEM((n * kv_rows // 2, kv_width), jnp.bfloat16),
            pltpu.VMEM((n * kv_rows // 2, kv_width), jnp.bfloat16),
        ],
        name="attend",
    )(meta, lengths, *low, *ups, *kvs, cosine, sine, q_base)


def row_length(mesh):
    line = mesh.devices[0, :, 0]
    level = line[0].coords[2]
    count = 1
    while count < line.size and line[count].coords[2] == level:
        count += 1
    return count


def solution(mesh):
    n, tp_size = mesh.shape["ctx"], mesh.shape["tp"]
    x_size = row_length(mesh)

    def shards(*args):
        hidden, q_base, adapter_down = args[:3]
        unit = n * LANES
        whole_blocks = hidden.shape[1] % (tp_size * unit) == 0 and q_base.shape[1] % unit == 0
        if n % x_size == 0 and whole_blocks:
            return shards_two_level(x_size, 2, *args)
        return shards_any(*args)

    return jax.shard_map(
        shards,
        mesh=mesh,
        in_specs=(
            P(("group", "ctx"), None),
            P(("group", "ctx"), "tp"),
            P(("group", "ctx"), None, None),
            P(("group", "ctx"), None, "tp"),
            P("group"),
            P("group"),
            P("group"),
            P(("group", "ctx"), "tp"),
            P(("group", "ctx"), "tp"),
            P(("group", "ctx"), "tp"),
            P(("group", "ctx"), "tp"),
        ),
        out_specs=P(("group", "ctx"), "tp"),
        check_vma=False,
    )
```

```python
import functools
import math

import jax
import jax.numpy as jnp
from jax import lax
from jax.experimental import pallas as pl
from jax.experimental.pallas import tpu as pltpu
from jax.sharding import PartitionSpec as P


HEAD_SIZE = 128
LANES = 128


def rotary_tables(token_positions):
    half_dim = HEAD_SIZE // 2
    inverse = jnp.exp(
        jnp.arange(half_dim, dtype=jnp.float32) * (-2.0 * math.log(500000.0) / HEAD_SIZE)
    )
    angles = token_positions.astype(jnp.float32)[:, None] * inverse[None, :]
    return jnp.cos(angles), jnp.sin(angles)


def spread(shard, axis, root):
    mine = lax.axis_index(axis) == root
    return lax.psum(jnp.where(mine, shard, jnp.zeros_like(shard)), axis)


def apply_rotary(values, token_positions, heads):
    half_dim = HEAD_SIZE // 2
    cosine, sine = rotary_tables(token_positions)
    cosine, sine = cosine[:, None, :], sine[:, None, :]
    shaped = values.reshape(values.shape[0], heads, HEAD_SIZE)
    first = shaped[..., :half_dim]
    second = shaped[..., half_dim:]
    turned = jnp.concatenate(
        [first * cosine - second * sine, second * cosine + first * sine], axis=-1
    )
    return turned.reshape(values.shape[0], heads * HEAD_SIZE)


def shards_any(
    hidden,
    q_base,
    adapter_down,
    adapter_up,
    adapter_owner,
    turn_start,
    shard_lengths,
    stored_keys,
    stored_values,
    unrotated_turn_keys,
    incoming_values,
):
    holder = adapter_owner[0]
    got_down, got_up = (
        spread(adapter_down[0], "ctx", holder),
        spread(adapter_up[0], "ctx", holder),
    )
    lowrank = jnp.dot(hidden, got_down, preferred_element_type=jnp.float32).astype(jnp.bfloat16)
    adapter_delta = jnp.dot(lowrank, got_up, preferred_element_type=jnp.float32)
    token_count = q_base.shape[0]
    slot_count = stored_keys.shape[0]
    shard_rows = token_count + slot_count
    ctx_size = lax.axis_size("ctx")
    myself = lax.axis_index("ctx")
    query_heads = q_base.shape[1] // HEAD_SIZE
    kv_heads = unrotated_turn_keys.shape[1] // HEAD_SIZE
    groups = query_heads // kv_heads
    local_tokens = jnp.arange(token_count, dtype=jnp.int32)
    token_positions = turn_start[0] + myself * token_count + local_tokens
    query_rows = apply_rotary(
        q_base.astype(jnp.float32) + 0.5 * adapter_delta, token_positions, query_heads
    ).astype(jnp.bfloat16)
    rotated_turn_keys = apply_rotary(
        unrotated_turn_keys.astype(jnp.float32), token_positions, kv_heads
    ).astype(jnp.bfloat16)
    grouped = query_rows.reshape(token_count, kv_heads, groups, HEAD_SIZE)
    key_here = jnp.concatenate([stored_keys, rotated_turn_keys], axis=0)
    value_here = jnp.concatenate([stored_values, incoming_values], axis=0)
    mine = myself * token_count + local_tokens
    score_scale = 1.0 / math.sqrt(HEAD_SIZE)
    shard_ids = jnp.arange(ctx_size, dtype=jnp.int32)

    def absorb(state, key_block, value_block, start):
        highest, denominator, accum = state
        row_count = key_block.shape[0]
        global_rows = start + jnp.arange(row_count, dtype=jnp.int32)
        owner_shard = global_rows // shard_rows
        within = global_rows % shard_rows
        is_cache = within < slot_count
        lengths_here = jnp.sum(
            jnp.where(owner_shard[:, None] == shard_ids[None, :], shard_lengths[None, :], 0), axis=1
        )
        token_number = owner_shard * token_count + (within - slot_count)
        allowed = jnp.where(
            is_cache[None, :],
            (within < lengths_here)[None, :],
            token_number[None, :] <= mine[:, None],
        )
        allowed = allowed[:, None, None, :]
        key_head_rows = key_block.reshape(-1, kv_heads, HEAD_SIZE)
        value_head_rows = value_block.reshape(-1, kv_heads, HEAD_SIZE)
        scores = (
            jnp.einsum("rhgd,khd->rhgk", grouped, key_head_rows, preferred_element_type=jnp.float32)
            * score_scale
        )
        new_high = jnp.maximum(highest, jnp.max(jnp.where(allowed, scores, -1e30), axis=-1))
        weights = jnp.where(allowed, jnp.exp(scores - new_high[..., None]), 0.0)
        fade = jnp.exp(highest - new_high)
        denominator = denominator * fade + jnp.sum(weights, axis=-1)
        product = jnp.einsum(
            "rhgk,khd->rhgd",
            weights.astype(jnp.bfloat16),
            value_head_rows,
            preferred_element_type=jnp.float32,
        )
        accum = accum * fade[..., None] + product
        return (new_high, denominator, accum)

    state = (
        jnp.full((token_count, kv_heads, groups), -1e30, jnp.float32),
        jnp.zeros((token_count, kv_heads, groups), jnp.float32),
        jnp.zeros((token_count, kv_heads, groups, HEAD_SIZE), jnp.float32),
    )
    block_rows = shard_rows * 8
    keys = lax.all_gather(key_here, "ctx", axis=0, tiled=True)
    values = lax.all_gather(value_here, "ctx", axis=0, tiled=True)
    row_count = keys.shape[0]
    if row_count > block_rows and row_count % block_rows == 0:
        count = row_count // block_rows
        key_split = keys.reshape(count, block_rows, keys.shape[1])
        value_split = values.reshape(count, block_rows, values.shape[1])

        def inner(carry, items):
            key_one, value_one, number = items
            return (absorb(carry, key_one, value_one, number * block_rows), None)

        numbers = jnp.arange(count, dtype=jnp.int32)
        state, _ = lax.scan(inner, state, (key_split, value_split, numbers))
    else:
        state = absorb(state, keys, values, jnp.int32(0))
    _, denominator, accum = state
    attended = accum / denominator[..., None]
    return attended.reshape(token_count, query_heads * HEAD_SIZE).astype(jnp.bfloat16)


QUAD = 4


def pack_kernel(cos_ref, sin_ref, sk_ref, sv_ref, tk_ref, tv_ref, kv_ref):
    slots, width = sk_ref.shape
    tokens = tk_ref.shape[0]
    rows = slots + tokens
    kv_ref[0:slots, :] = sk_ref[...]
    kv_ref[rows : rows + slots, :] = sv_ref[...]
    kv_ref[rows + slots : 2 * rows, :] = tv_ref[...]
    cosine, sine = cos_ref[...], sin_ref[...]
    for h in range(width // HEAD_SIZE):
        at = slice(h * HEAD_SIZE, (h + 1) * HEAD_SIZE)
        v = tk_ref[:, at].astype(jnp.float32)
        turned = v * cosine + pltpu.roll(v, HEAD_SIZE // 2, 1) * sine
        kv_ref[slots:rows, at] = turned.astype(kv_ref.dtype)


def copy_all(jobs, sems):
    for i, options in enumerate(jobs):
        free = None
        for condition, source, target in options:
            if condition is None:
                now = free
            else:
                now = condition if free is None else free & condition
                free = ~condition if free is None else free & ~condition
            copy = pltpu.make_async_copy(source, target, sems.at[i])
            if now is None:
                copy.start()
            else:
                pl.when(now)(copy.start)
    for i, options in enumerate(jobs):
        condition, source, target = options[-1]
        pltpu.make_async_copy(source, target, sems.at[i]).wait()


def down_at(pos_ref, down_ref, wide, half, other_z, other_x):
    step = down_ref.shape[0] // 2
    part = (pos_ref[0] * 2 + (pos_ref[1] ^ other_z)) * 2 + (pos_ref[2] ^ other_x)
    at = pl.multiple_of(part * wide, LANES)
    return down_ref.at[half * step : (half + 1) * step, pl.ds(at, wide)]


def hidden_at(pos_ref, hidden_ref, wide, other_z, other_x):
    part = (pos_ref[0] * 2 + (pos_ref[1] ^ other_z)) * 2 + (pos_ref[2] ^ other_x)
    at = pl.multiple_of(part * wide, LANES)
    return hidden_ref.at[:, pl.ds(at, wide)]


def up_at(pos_ref, up_ref, half, piece, other_z, other_x):
    step = up_ref.shape[0] // 4
    columns = up_ref.shape[1] // QUAD
    part = (pos_ref[1] ^ other_z) * 2 + (pos_ref[2] ^ other_x)
    at = pl.multiple_of(part * columns, LANES)
    row = (2 * half + piece) * step
    return up_ref.at[row : row + step, pl.ds(at, columns)]


def packed_down(ref, rank):
    return ref.at[0 : rank // 2]


def packed_up(ref, rank, piece):
    columns = ref.shape[1] // 2
    return ref.at[rank // 2 : rank // 2 + rank // 4, piece * columns : (piece + 1) * columns]


def first_kernel(pos_ref, down_ref, up_ref, hidden_ref, sx_ref, sz_ref, hz_ref, sems):
    rank = down_ref.shape[0]
    wide = sx_ref.shape[2]
    jobs = []
    for j in range(2):
        jobs.append([(None, hidden_at(pos_ref, hidden_ref, wide, 1, j), hz_ref.at[j])])
    for half, ref in ((0, sx_ref), (1, sz_ref)):
        for j in range(2):
            oz, ox = (j, 1) if half == 0 else (1, j)
            jobs.append(
                [(None, down_at(pos_ref, down_ref, wide, half, oz, ox), packed_down(ref.at[j], rank))]
            )
            for piece in range(2):
                jobs.append(
                    [(None, up_at(pos_ref, up_ref, half, piece, oz, ox), packed_up(ref.at[j], rank, piece))]
                )
    copy_all(jobs, sems)


def second_kernel(pos_ref, down_ref, up_ref, rx_ref, rz_ref, sz_ref, sx_ref, sems):
    rank = down_ref.shape[0]
    wide = sx_ref.shape[1]
    z_differs, x_differs = pos_ref[3] == 1, pos_ref[4] == 1
    jobs = []
    for half, got, ref, oz, ox, differs in (
        (0, rx_ref, sz_ref, 1, 0, x_differs),
        (1, rz_ref, sx_ref, 0, 1, z_differs),
    ):
        jobs.append(
            [
                (differs, packed_down(got.at[1], rank), packed_down(ref, rank)),
                (None, down_at(pos_ref, down_ref, wide, half, oz, ox), packed_down(ref, rank)),
            ]
        )
        for piece in range(2):
            target = packed_up(ref, rank, piece)
            jobs.append(
                [
                    (differs, packed_up(got.at[1], rank, piece), target),
                    (None, up_at(pos_ref, up_ref, half, piece, oz, ox), target),
                ]
            )
    copy_all(jobs, sems)


def hidden_kernel(pos_ref, hidden_ref, gz_ref, hx_ref, hf_ref, sems):
    wide = hx_ref.shape[2]
    copy_all(
        [
            [(None, hidden_at(pos_ref, hidden_ref, wide, 0, 1), hx_ref.at[0])],
            [(None, hidden_at(pos_ref, hidden_ref, wide, 0, 0), hf_ref.at[0])],
            [(None, gz_ref.at[1], hx_ref.at[1])],
            [(None, gz_ref.at[0], hf_ref.at[1])],
        ],
        sems,
    )


def up_kernel(pos_ref, up_ref, rx_ref, rz_ref, r2z_ref, r2x_ref, out_ref, sems):
    rank = up_ref.shape[0]
    step = rank // 4
    z_differs, x_differs = pos_ref[3] == 1, pos_ref[4] == 1
    jobs = []
    for half in range(2):
        for piece in range(2):
            row = (2 * half + piece) * step
            target = out_ref.at[row : row + step]
            late, early = (r2z_ref, rx_ref) if half == 0 else (r2x_ref, rz_ref)
            one, two = (z_differs, x_differs) if half == 0 else (x_differs, z_differs)
            jobs.append(
                [
                    (one, packed_up(late, rank, piece), target),
                    (two, packed_up(early.at[0], rank, piece), target),
                    (None, up_at(pos_ref, up_ref, half, piece, 0, 0), target),
                ]
            )
    copy_all(jobs, sems)


def lowrank_kernel(
    far, pos_ref, down_ref, rx_ref, rz_ref, r2z_ref, r2x_ref, *refs
):
    count = 2 * far
    hid = refs[:count]
    keep_ref, send_ref, a_ref, h_ref, sems = refs[count:]
    rank, wide = a_ref.shape
    z_differs, x_differs = pos_ref[3] == 1, pos_ref[4] == 1
    jobs = []
    for half in range(2):
        target = a_ref.at[half * (rank // 2) : (half + 1) * (rank // 2)]
        late, early = (r2z_ref, rx_ref) if half == 0 else (r2x_ref, rz_ref)
        one, two = (z_differs, x_differs) if half == 0 else (x_differs, z_differs)
        jobs.append(
            [
                (one, packed_down(late, rank), target),
                (two, packed_down(early.at[0], rank), target),
                (None, down_at(pos_ref, down_ref, wide, half, 0, 0), target),
            ]
        )
    tokens = hid[0].shape[1]
    for i in range(count):
        for j in range(2):
            at = (2 * i + j) * tokens
            h_ref[at : at + tokens, :] = hid[i][j]
    copy_all(jobs, sems)
    p = lax.dot_general(
        h_ref[...], a_ref[...], (((1,), (1,)), ((), ())), preferred_element_type=jnp.float32
    )
    for i in range(count):
        out = keep_ref if i < far else send_ref
        for j in range(2):
            at = (2 * i + j) * tokens
            out[j, i % far] = p[at : at + tokens]


def attend_kernel(far, slots, meta_ref, len_ref, *refs):
    low = refs[:far]
    ups = refs[far : far + QUAD]
    kvs = refs[far + QUAD : far + QUAD + 3]
    cos_ref, sin_ref, q_ref, o_ref, d_ref, qs_ref, k_ref, v_ref, low_ref = refs[far + QUAD + 3 :]
    n = QUAD * far
    tokens = q_ref.shape[0]
    rows = kvs[0].shape[1] // 2
    width = d_ref.shape[2]
    query_heads = q_ref.shape[1] // HEAD_SIZE
    kv_heads = k_ref.shape[1] // HEAD_SIZE
    groups = query_heads // kv_heads
    myself, pick = meta_ref[0], meta_ref[1]
    for s in range(far):

        @pl.when(pick == s)
        def _(s=s):
            low_ref[...] = low[s][...]

    lowrank = low_ref[...].astype(jnp.bfloat16)
    for i in range(QUAD):
        d_ref[meta_ref[2 + i]] = jnp.dot(lowrank, ups[i][...], preferred_element_type=jnp.float32)
    pieces = [kvs[0].at[s] for s in range(far)] + [kvs[1].at[s] for s in range(far)]
    pieces += [kvs[2].at[s] for s in range(2 * far)]
    for i, piece in enumerate(pieces):
        k_ref[i * rows : (i + 1) * rows, :] = piece[0:rows, :]
        v_ref[i * rows : (i + 1) * rows, :] = piece[rows : 2 * rows, :]
    cosine, sine = cos_ref[...], sin_ref[...]
    for h in range(query_heads):
        b, off = divmod(h * HEAD_SIZE, width)
        v = q_ref[:, h * HEAD_SIZE : (h + 1) * HEAD_SIZE].astype(jnp.float32)
        v = v + 0.5 * d_ref[b, :, off : off + HEAD_SIZE]
        turned = v * cosine + pltpu.roll(v, HEAD_SIZE // 2, 1) * sine
        g = h % groups
        qs_ref[h // groups, g * tokens : (g + 1) * tokens, :] = turned.astype(jnp.bfloat16)
    shape = (tokens, n * rows)
    col = lax.broadcasted_iota(jnp.int32, shape, 1)
    token = myself * tokens + lax.broadcasted_iota(jnp.int32, shape, 0)
    start = jnp.zeros(shape, jnp.int32)
    limit = jnp.zeros(shape, jnp.int32)
    first = jnp.zeros(shape, jnp.int32)
    for i in range(n):
        after = col >= i * rows
        start = jnp.where(after, i * rows, start)
        limit = jnp.where(after, len_ref[i], limit)
        first = jnp.where(after, meta_ref[2 + QUAD + i] * tokens, first)
    within = col - start
    ok = jnp.where(within < slots, within - limit, within - slots + first - token - 1) < 0
    bias = jnp.where(ok, 0.0, -1e30)[None]
    scale = 1.0 / math.sqrt(HEAD_SIZE)
    for kv in range(kv_heads):
        at = slice(kv * HEAD_SIZE, (kv + 1) * HEAD_SIZE)
        s = lax.dot_general(
            qs_ref[kv], k_ref[:, at], (((1,), (1,)), ((), ())), preferred_element_type=jnp.float32
        )
        s = s.reshape(groups, tokens, n * rows) * scale + bias
        w = jnp.exp(s - jnp.max(s, axis=-1, keepdims=True))
        denominator = jnp.sum(w, axis=-1, keepdims=True)
        w = w.reshape(groups * tokens, n * rows).astype(jnp.bfloat16)
        o = jnp.dot(w, v_ref[:, at], preferred_element_type=jnp.float32)
        o = o.reshape(groups, tokens, HEAD_SIZE) / denominator
        for g in range(groups):
            h = kv * groups + g
            o_ref[:, h * HEAD_SIZE : (h + 1) * HEAD_SIZE] = o[g].astype(o_ref.dtype)


def specs(space, count):
    return [pl.BlockSpec(memory_space=space)] * count


def call(kernel, shapes, inputs, outputs, scratch=()):
    return pl.pallas_call(
        kernel,
        out_shape=[jax.ShapeDtypeStruct(s, d) for s, d in shapes],
        in_specs=inputs,
        out_specs=outputs,
        scratch_shapes=list(scratch),
    )


def shards_quads(
    hidden,
    q_base,
    adapter_down,
    adapter_up,
    adapter_owner,
    turn_start,
    shard_lengths,
    stored_keys,
    stored_values,
    unrotated_turn_keys,
    incoming_values,
):
    n = lax.axis_size("ctx")
    tp_size = lax.axis_size("tp")
    far = n // QUAD
    myself = lax.axis_index("ctx")
    core = lax.axis_index("tp")
    quad, zl, x = myself // QUAD, myself // 2 % 2, myself % 2
    owner = adapter_owner[0]
    owner_quad, owner_zl, owner_x = owner // QUAD, owner // 2 % 2, owner % 2
    tokens, features = hidden.shape
    wide = features // (tp_size * QUAD)
    rank = adapter_down.shape[2]
    columns = adapter_up.shape[2]
    quarter = columns // QUAD
    slots, kv_width = stored_keys.shape
    bf16, f32 = jnp.bfloat16, jnp.float32
    smem, vmem, anywhere = pltpu.SMEM, pltpu.VMEM, pl.ANY

    def permute(v, flip=0, shift=0, core_shift=0):
        pairs = []
        for a in range(n):
            to = (a // QUAD + shift) % far * QUAD + (a % QUAD ^ flip)
            for c in range(tp_size):
                pairs.append((a * tp_size + c, to * tp_size + (c + core_shift) % tp_size))
        return lax.ppermute(v, ("ctx", "tp"), pairs)

    down, up = adapter_down[0].T, adapter_up[0]
    pos = jnp.stack(
        [
            core,
            zl,
            x,
            (zl != owner_zl).astype(jnp.int32),
            (x != owner_x).astype(jnp.int32),
        ]
    )
    packed = rank // 2 + rank // 4

    sx, sz, hz = call(
        first_kernel,
        [((2, packed, wide), bf16), ((2, packed, wide), bf16), ((2, tokens, wide), bf16)],
        specs(smem, 1) + specs(anywhere, 3),
        specs(anywhere, 3),
        [pltpu.SemaphoreType.DMA((14,))],
    )(pos, down, up, hidden)
    gz = permute(hz, 2)
    rx = permute(sx, 1)
    rz = permute(sz, 2)

    hx, hf = call(
        hidden_kernel,
        [((2, tokens, wide), bf16), ((2, tokens, wide), bf16)],
        specs(smem, 1) + specs(anywhere, 2),
        specs(anywhere, 2),
        [pltpu.SemaphoreType.DMA((4,))],
    )(pos, hidden, gz)
    hg = permute(hx, 1)
    hid = [hf] + [permute(hf, 0, s) for s in range(1, far)]
    hid += [hg] + [permute(hg, 0, s) for s in range(1, far)]

    s2z, s2x = call(
        second_kernel,
        [((packed, wide), bf16), ((packed, wide), bf16)],
        specs(smem, 1) + specs(anywhere, 4),
        specs(anywhere, 2),
        [pltpu.SemaphoreType.DMA((6,))],
    )(pos, down, up, rx, rz)
    r2z = permute(s2z, 2)
    r2x = permute(s2x, 1)

    (mine,) = call(
        up_kernel,
        [((rank, quarter), bf16)],
        specs(smem, 1) + specs(anywhere, 5),
        specs(anywhere, 1),
        [pltpu.SemaphoreType.DMA((4,))],
    )(pos, up, rx, rz, r2z, r2x)
    quarters = mine
    for s in range(1, far):
        came = permute(mine, 0, s)
        quarters = jnp.where((quad - owner_quad) % far == s, came, quarters)
    up_z = permute(quarters, 2)
    up_x = permute(quarters, 1)
    up_zx = permute(up_z, 1)

    partial_shape = ((2, far, tokens, rank), f32)
    keep, send = call(
        functools.partial(lowrank_kernel, far),
        [partial_shape, partial_shape],
        specs(smem, 1) + specs(anywhere, 5) + specs(vmem, 2 * far),
        specs(vmem, 2),
        [
            pltpu.VMEM((rank, wide), bf16),
            pltpu.VMEM((n * tokens, wide), bf16),
            pltpu.SemaphoreType.DMA((2,)),
        ],
    )(pos, down, rx, rz, r2z, r2x, *hid)
    total = keep
    for c in range(tp_size):
        total = total + permute(send, 1, 0, c)
        if c:
            total = total + permute(keep, 0, 0, c)
    total = total[0] + permute(total[1], 2)
    low = [total[0]] + [permute(total[s], 0, -s) for s in range(1, far)]

    positions = turn_start[0] + myself * tokens + jnp.arange(tokens, dtype=jnp.int32)
    cosine, sine = rotary_tables(positions)
    cosine = jnp.concatenate([cosine, cosine], axis=1)
    sine = jnp.concatenate([-sine, sine], axis=1)
    kv_rows = 2 * (slots + tokens)
    (kv,) = call(pack_kernel, [((kv_rows, kv_width), bf16)], specs(vmem, 6), specs(vmem, 1))(
        cosine, sine, stored_keys, stored_values, unrotated_turn_keys, incoming_values
    )
    kv = jnp.stack([kv] + [permute(kv, 0, s) for s in range(1, far)])
    kv_z = permute(kv, 2)
    kv_x = permute(jnp.concatenate([kv, kv_z]), 1)

    places = [(s, dz, dx) for dx in range(2) for dz in range(2) for s in range(far)]
    ids = [((quad - s) % far * 2 + (zl ^ dz)) * 2 + (x ^ dx) for s, dz, dx in places]
    blocks = [(zl ^ dz) * 2 + (x ^ dx) for dz, dx in ((0, 0), (1, 0), (0, 1), (1, 1))]
    meta = jnp.stack([myself, (owner_quad - quad) % far] + blocks + ids)
    lengths = shard_lengths[jnp.stack(ids)]
    (out,) = call(
        functools.partial(attend_kernel, far, slots),
        [(q_base.shape, bf16)],
        specs(smem, 2) + specs(vmem, far + QUAD + 6),
        specs(vmem, 1),
        [
            pltpu.VMEM((QUAD, tokens, quarter), f32),
            pltpu.VMEM((kv_width // HEAD_SIZE, columns // kv_width * tokens, HEAD_SIZE), bf16),
            pltpu.VMEM((n * kv_rows // 2, kv_width), bf16),
            pltpu.VMEM((n * kv_rows // 2, kv_width), bf16),
            pltpu.VMEM((tokens, rank), f32),
        ],
    )(meta, lengths, *low, quarters, up_z, up_x, up_zx, kv, kv_z, kv_x, cosine, sine, q_base)
    return out


def fits_quads(mesh, hidden, q_base, adapter_down, stored_keys):
    n, tp_size = mesh.shape["ctx"], mesh.shape["tp"]
    if n % QUAD or n == QUAD:
        return False
    wide_whole = hidden.shape[1] % (tp_size * QUAD * LANES) == 0
    quarter_whole = q_base.shape[1] % (QUAD * LANES) == 0
    packs = adapter_down.shape[2] % 64 == 0 and hidden.shape[1] // tp_size == 2 * q_base.shape[1]
    rows = n * (stored_keys.shape[0] + q_base.shape[0])
    kv_width = stored_keys.shape[1]
    queries = q_base.shape[1] // kv_width * q_base.shape[0]
    room = rows * (8 * kv_width + 12 * queries)
    return wide_whole and quarter_whole and packs and room < 16 * 2**20


def solution(mesh):
    def shards(*args):
        hidden, q_base, adapter_down, stored_keys = args[0], args[1], args[2], args[7]
        if fits_quads(mesh, hidden, q_base, adapter_down, stored_keys):
            return shards_quads(*args)
        return shards_any(*args)

    return jax.shard_map(
        shards,
        mesh=mesh,
        in_specs=(
            P(("group", "ctx"), None),
            P(("group", "ctx"), "tp"),
            P(("group", "ctx"), None, None),
            P(("group", "ctx"), None, "tp"),
            P("group"),
            P("group"),
            P("group"),
            P(("group", "ctx"), "tp"),
            P(("group", "ctx"), "tp"),
            P(("group", "ctx"), "tp"),
            P(("group", "ctx"), "tp"),
        ),
        out_specs=P(("group", "ctx"), "tp"),
        check_vma=False,
    )
```

```python
import functools
import math

import jax
import jax.numpy as jnp
from jax import lax
from jax.experimental import pallas as pl
from jax.experimental.pallas import tpu as pltpu
from jax.sharding import PartitionSpec as P


HEAD_SIZE = 128
LANES = 128


def rotary_tables(token_positions):
    half_dim = HEAD_SIZE // 2
    inverse = jnp.exp(
        jnp.arange(half_dim, dtype=jnp.float32) * (-2.0 * math.log(500000.0) / HEAD_SIZE)
    )
    angles = token_positions.astype(jnp.float32)[:, None] * inverse[None, :]
    return jnp.cos(angles), jnp.sin(angles)


def spread(shard, axis, root):
    mine = lax.axis_index(axis) == root
    return lax.psum(jnp.where(mine, shard, jnp.zeros_like(shard)), axis)


def apply_rotary(values, token_positions, heads):
    half_dim = HEAD_SIZE // 2
    cosine, sine = rotary_tables(token_positions)
    cosine, sine = cosine[:, None, :], sine[:, None, :]
    shaped = values.reshape(values.shape[0], heads, HEAD_SIZE)
    first = shaped[..., :half_dim]
    second = shaped[..., half_dim:]
    turned = jnp.concatenate(
        [first * cosine - second * sine, second * cosine + first * sine], axis=-1
    )
    return turned.reshape(values.shape[0], heads * HEAD_SIZE)


def shards_any(
    hidden,
    q_base,
    adapter_down,
    adapter_up,
    adapter_owner,
    turn_start,
    shard_lengths,
    stored_keys,
    stored_values,
    unrotated_turn_keys,
    incoming_values,
):
    holder = adapter_owner[0]
    got_down, got_up = (
        spread(adapter_down[0], "ctx", holder),
        spread(adapter_up[0], "ctx", holder),
    )
    lowrank = jnp.dot(hidden, got_down, preferred_element_type=jnp.float32).astype(jnp.bfloat16)
    adapter_delta = jnp.dot(lowrank, got_up, preferred_element_type=jnp.float32)
    token_count = q_base.shape[0]
    slot_count = stored_keys.shape[0]
    shard_rows = token_count + slot_count
    ctx_size = lax.axis_size("ctx")
    myself = lax.axis_index("ctx")
    query_heads = q_base.shape[1] // HEAD_SIZE
    kv_heads = unrotated_turn_keys.shape[1] // HEAD_SIZE
    groups = query_heads // kv_heads
    local_tokens = jnp.arange(token_count, dtype=jnp.int32)
    token_positions = turn_start[0] + myself * token_count + local_tokens
    query_rows = apply_rotary(
        q_base.astype(jnp.float32) + 0.5 * adapter_delta, token_positions, query_heads
    ).astype(jnp.bfloat16)
    rotated_turn_keys = apply_rotary(
        unrotated_turn_keys.astype(jnp.float32), token_positions, kv_heads
    ).astype(jnp.bfloat16)
    grouped = query_rows.reshape(token_count, kv_heads, groups, HEAD_SIZE)
    key_here = jnp.concatenate([stored_keys, rotated_turn_keys], axis=0)
    value_here = jnp.concatenate([stored_values, incoming_values], axis=0)
    mine = myself * token_count + local_tokens
    score_scale = 1.0 / math.sqrt(HEAD_SIZE)
    shard_ids = jnp.arange(ctx_size, dtype=jnp.int32)

    def absorb(state, key_block, value_block, start):
        highest, denominator, accum = state
        row_count = key_block.shape[0]
        global_rows = start + jnp.arange(row_count, dtype=jnp.int32)
        owner_shard = global_rows // shard_rows
        within = global_rows % shard_rows
        is_cache = within < slot_count
        lengths_here = jnp.sum(
            jnp.where(owner_shard[:, None] == shard_ids[None, :], shard_lengths[None, :], 0), axis=1
        )
        token_number = owner_shard * token_count + (within - slot_count)
        allowed = jnp.where(
            is_cache[None, :],
            (within < lengths_here)[None, :],
            token_number[None, :] <= mine[:, None],
        )
        allowed = allowed[:, None, None, :]
        key_head_rows = key_block.reshape(-1, kv_heads, HEAD_SIZE)
        value_head_rows = value_block.reshape(-1, kv_heads, HEAD_SIZE)
        scores = (
            jnp.einsum("rhgd,khd->rhgk", grouped, key_head_rows, preferred_element_type=jnp.float32)
            * score_scale
        )
        new_high = jnp.maximum(highest, jnp.max(jnp.where(allowed, scores, -1e30), axis=-1))
        weights = jnp.where(allowed, jnp.exp(scores - new_high[..., None]), 0.0)
        fade = jnp.exp(highest - new_high)
        denominator = denominator * fade + jnp.sum(weights, axis=-1)
        product = jnp.einsum(
            "rhgk,khd->rhgd",
            weights.astype(jnp.bfloat16),
            value_head_rows,
            preferred_element_type=jnp.float32,
        )
        accum = accum * fade[..., None] + product
        return (new_high, denominator, accum)

    state = (
        jnp.full((token_count, kv_heads, groups), -1e30, jnp.float32),
        jnp.zeros((token_count, kv_heads, groups), jnp.float32),
        jnp.zeros((token_count, kv_heads, groups, HEAD_SIZE), jnp.float32),
    )
    block_rows = shard_rows * 8
    keys = lax.all_gather(key_here, "ctx", axis=0, tiled=True)
    values = lax.all_gather(value_here, "ctx", axis=0, tiled=True)
    row_count = keys.shape[0]
    if row_count > block_rows and row_count % block_rows == 0:
        count = row_count // block_rows
        key_split = keys.reshape(count, block_rows, keys.shape[1])
        value_split = values.reshape(count, block_rows, values.shape[1])

        def inner(carry, items):
            key_one, value_one, number = items
            return (absorb(carry, key_one, value_one, number * block_rows), None)

        numbers = jnp.arange(count, dtype=jnp.int32)
        state, _ = lax.scan(inner, state, (key_split, value_split, numbers))
    else:
        state = absorb(state, keys, values, jnp.int32(0))
    _, denominator, accum = state
    attended = accum / denominator[..., None]
    return attended.reshape(token_count, query_heads * HEAD_SIZE).astype(jnp.bfloat16)


QUAD = 4


def pack_kernel(cos_ref, sin_ref, sk_ref, sv_ref, tk_ref, tv_ref, kv_ref):
    slots, width = sk_ref.shape
    tokens = tk_ref.shape[0]
    rows = slots + tokens
    kv_ref[0:slots, :] = sk_ref[...]
    kv_ref[rows : rows + slots, :] = sv_ref[...]
    kv_ref[rows + slots : 2 * rows, :] = tv_ref[...]
    cosine, sine = cos_ref[...], sin_ref[...]
    for h in range(width // HEAD_SIZE):
        at = slice(h * HEAD_SIZE, (h + 1) * HEAD_SIZE)
        v = tk_ref[:, at].astype(jnp.float32)
        turned = v * cosine + pltpu.roll(v, HEAD_SIZE // 2, 1) * sine
        kv_ref[slots:rows, at] = turned.astype(kv_ref.dtype)


def place():
    myself = lax.axis_index("ctx")
    return lax.axis_index("tp"), myself // QUAD, myself // 2 % 2, myself % 2


def differs(owner_ref):
    _, _, zl, x = place()
    owner = owner_ref[0]
    return owner // 2 % 2 != zl, owner % 2 != x


def start_all(pairs, sems):
    copies = [pltpu.make_async_copy(a, b, sems.at[i]) for i, (a, b) in enumerate(pairs)]
    for copy in copies:
        copy.start()
    for copy in copies:
        copy.wait()


def feature_part(wide, other_z, other_x):
    core, _, zl, x = place()
    part = (core * 2 + (zl ^ other_z)) * 2 + (x ^ other_x)
    return pl.ds(pl.multiple_of(part * wide, LANES), wide)


def factor_pairs(down_ref, up_ref, target, half, other_z, other_x):
    rank = down_ref.shape[0]
    wide = target.shape[1]
    columns = up_ref.shape[1] // QUAD
    _, _, zl, x = place()
    part = (zl ^ other_z) * 2 + (x ^ other_x)
    at = pl.ds(pl.multiple_of(part * columns, LANES), columns)
    top, step = rank // 2, rank // 4
    pairs = [
        (
            down_ref.at[half * top : (half + 1) * top, feature_part(wide, other_z, other_x)],
            target.at[0:top],
        )
    ]
    for piece in range(2):
        row = (2 * half + piece) * step
        pairs.append(
            (
                up_ref.at[row : row + step, at],
                target.at[top : top + step, piece * columns : (piece + 1) * columns],
            )
        )
    return pairs


def first_kernel(down_ref, up_ref, hidden_ref, sx_ref, sz_ref, hz_ref, sems):
    wide = sx_ref.shape[2]
    pairs = []
    for j in range(2):
        pairs.append((hidden_ref.at[:, feature_part(wide, 1, j)], hz_ref.at[j]))
    for j in range(2):
        pairs += factor_pairs(down_ref, up_ref, sx_ref.at[j], 0, j, 1)
    for j in range(2):
        pairs += factor_pairs(down_ref, up_ref, sz_ref.at[j], 1, 1, j)
    start_all(pairs, sems)


def own_kernel(down_ref, up_ref, hidden_ref, ox_ref, oz_ref, hh_ref, sems):
    wide = ox_ref.shape[2]
    pairs = []
    for j in range(2):
        pairs.append((hidden_ref.at[:, feature_part(wide, 0, j)], hh_ref.at[j]))
    for j in range(2):
        pairs += factor_pairs(down_ref, up_ref, ox_ref.at[j], 0, j, 0)
    for j in range(2):
        pairs += factor_pairs(down_ref, up_ref, oz_ref.at[j], 1, 0, j)
    start_all(pairs, sems)


def hidden_kernel(hh_ref, gz_ref, hx_ref, hf_ref):
    hx_ref[0] = hh_ref[1]
    hx_ref[1] = gz_ref[1]
    hf_ref[0] = hh_ref[0]
    hf_ref[1] = gz_ref[0]


def second_kernel(owner_ref, ox_ref, oz_ref, rx_ref, rz_ref, sz_ref, sx_ref):
    z_differs, x_differs = differs(owner_ref)

    @pl.when(x_differs)
    def _():
        sz_ref[...] = rx_ref[1]

    @pl.when(~x_differs)
    def _():
        sz_ref[...] = ox_ref[1]

    @pl.when(z_differs)
    def _():
        sx_ref[...] = rz_ref[1]

    @pl.when(~z_differs)
    def _():
        sx_ref[...] = oz_ref[1]


def choose_late(owner_ref, ox_ref, oz_ref, rx_ref, rz_ref, r2z_ref, r2x_ref, put):
    z_differs, x_differs = differs(owner_ref)
    for half, late, early, own, one, two in (
        (0, r2z_ref, rx_ref, ox_ref, z_differs, x_differs),
        (1, r2x_ref, rz_ref, oz_ref, x_differs, z_differs),
    ):
        pl.when(one)(functools.partial(put, half, late))
        pl.when(~one & two)(functools.partial(put, half, early.at[0]))
        pl.when(~one & ~two)(functools.partial(put, half, own.at[0]))


def up_kernel(owner_ref, *refs):
    out_ref = refs[6]
    rank, columns = out_ref.shape
    top, step = rank // 2, rank // 4

    def put(half, ref):
        for piece in range(2):
            row = (2 * half + piece) * step
            out_ref[row : row + step, :] = ref[
                top : top + step, piece * columns : (piece + 1) * columns
            ]

    choose_late(owner_ref, *refs[:6], put)


def lowrank_kernel(far, owner_ref, *refs):
    count = 2 * far
    hid = refs[6 : 6 + count]
    keep_ref, send_ref, a_ref, h_ref = refs[6 + count :]
    top = a_ref.shape[0] // 2

    def put(half, ref):
        a_ref[half * top : (half + 1) * top, :] = ref[0:top]

    choose_late(owner_ref, *refs[:6], put)
    tokens = hid[0].shape[1]
    for i in range(count):
        for j in range(2):
            at = (2 * i + j) * tokens
            h_ref[at : at + tokens, :] = hid[i][j]
    p = lax.dot_general(
        h_ref[...], a_ref[...], (((1,), (1,)), ((), ())), preferred_element_type=jnp.float32
    )
    for i in range(count):
        out = keep_ref if i < far else send_ref
        for j in range(2):
            at = (2 * i + j) * tokens
            out[j, i % far] = p[at : at + tokens]


def attend_kernel(far, slots, owner_ref, len_ref, *refs):
    low = refs[:far]
    ups = refs[far : far + QUAD]
    kvs = refs[far + QUAD : far + QUAD + 3]
    cos_ref, sin_ref, q_ref, o_ref, d_ref, qs_ref, k_ref, v_ref, low_ref = refs[far + QUAD + 3 :]
    n = QUAD * far
    tokens = q_ref.shape[0]
    rows = kvs[0].shape[1] // 2
    width = d_ref.shape[2]
    query_heads = q_ref.shape[1] // HEAD_SIZE
    kv_heads = k_ref.shape[1] // HEAD_SIZE
    groups = query_heads // kv_heads
    _, quad, zl, x = place()
    myself = lax.axis_index("ctx")
    pick = (owner_ref[0] // QUAD - quad + far) % far
    places = [(s, dz, dx) for dx in range(2) for dz in range(2) for s in range(far)]
    ids = [((quad - s + far) % far * 2 + (zl ^ dz)) * 2 + (x ^ dx) for s, dz, dx in places]
    blocks = [(zl ^ dz) * 2 + (x ^ dx) for dz, dx in ((0, 0), (1, 0), (0, 1), (1, 1))]
    for s in range(far):

        @pl.when(pick == s)
        def _(s=s):
            low_ref[...] = low[s][...]

    lowrank = low_ref[...].astype(jnp.bfloat16)
    for i in range(QUAD):
        d_ref[blocks[i]] = jnp.dot(lowrank, ups[i][...], preferred_element_type=jnp.float32)
    pieces = [kvs[0].at[s] for s in range(far)] + [kvs[1].at[s] for s in range(far)]
    pieces += [kvs[2].at[s] for s in range(2 * far)]
    for i, piece in enumerate(pieces):
        k_ref[i * rows : (i + 1) * rows, :] = piece[0:rows, :]
        v_ref[i * rows : (i + 1) * rows, :] = piece[rows : 2 * rows, :]
    cosine, sine = cos_ref[...], sin_ref[...]
    for h in range(query_heads):
        b, off = divmod(h * HEAD_SIZE, width)
        v = q_ref[:, h * HEAD_SIZE : (h + 1) * HEAD_SIZE].astype(jnp.float32)
        v = v + 0.5 * d_ref[b, :, off : off + HEAD_SIZE]
        turned = v * cosine + pltpu.roll(v, HEAD_SIZE // 2, 1) * sine
        g = h % groups
        qs_ref[h // groups, g * tokens : (g + 1) * tokens, :] = turned.astype(jnp.bfloat16)
    shape = (tokens, n * rows)
    col = lax.broadcasted_iota(jnp.int32, shape, 1)
    token = myself * tokens + lax.broadcasted_iota(jnp.int32, shape, 0)
    start = jnp.zeros(shape, jnp.int32)
    limit = jnp.zeros(shape, jnp.int32)
    first = jnp.zeros(shape, jnp.int32)
    for i in range(n):
        after = col >= i * rows
        start = jnp.where(after, i * rows, start)
        limit = jnp.where(after, len_ref[ids[i]], limit)
        first = jnp.where(after, ids[i] * tokens, first)
    within = col - start
    ok = jnp.where(within < slots, within - limit, within - slots + first - token - 1) < 0
    bias = jnp.where(ok, 0.0, -1e30)[None]
    scale = 1.0 / math.sqrt(HEAD_SIZE)
    for kv in range(kv_heads):
        at = slice(kv * HEAD_SIZE, (kv + 1) * HEAD_SIZE)
        s = lax.dot_general(
            qs_ref[kv], k_ref[:, at], (((1,), (1,)), ((), ())), preferred_element_type=jnp.float32
        )
        s = s.reshape(groups, tokens, n * rows) * scale + bias
        w = jnp.exp(s - jnp.max(s, axis=-1, keepdims=True))
        denominator = jnp.sum(w, axis=-1, keepdims=True)
        w = w.reshape(groups * tokens, n * rows).astype(jnp.bfloat16)
        o = jnp.dot(w, v_ref[:, at], preferred_element_type=jnp.float32)
        o = o.reshape(groups, tokens, HEAD_SIZE) / denominator
        for g in range(groups):
            h = kv * groups + g
            o_ref[:, h * HEAD_SIZE : (h + 1) * HEAD_SIZE] = o[g].astype(o_ref.dtype)


def specs(space, count):
    return [pl.BlockSpec(memory_space=space)] * count


def call(kernel, shapes, inputs, outputs, scratch=(), room=4 * 2**20, keep=True):
    out_shape = [(pltpu.VMEM if keep else jax.ShapeDtypeStruct)(s, d) for s, d in shapes]
    run = pl.pallas_call(
        kernel,
        out_shape=out_shape,
        in_specs=inputs,
        out_specs=outputs,
        scratch_shapes=list(scratch),
        compiler_params=pltpu.CompilerParams(vmem_limit_bytes=room),
    )

    def placed(*args):
        return run(
            *(
                pltpu.with_memory_space_constraint(a, i.memory_space)
                if i.memory_space in (pltpu.VMEM, pltpu.HBM)
                else a
                for a, i in zip(args, inputs, strict=True)
            )
        )

    return placed


def shards_quads(
    hidden,
    q_base,
    adapter_down,
    adapter_up,
    adapter_owner,
    turn_start,
    shard_lengths,
    stored_keys,
    stored_values,
    unrotated_turn_keys,
    incoming_values,
):
    n = lax.axis_size("ctx")
    tp_size = lax.axis_size("tp")
    far = n // QUAD
    myself = lax.axis_index("ctx")
    quad = myself // QUAD
    owner = adapter_owner[0]
    owner_quad = owner // QUAD
    tokens, features = hidden.shape
    wide = features // (tp_size * QUAD)
    rank = adapter_down.shape[2]
    columns = adapter_up.shape[2]
    quarter = columns // QUAD
    slots, kv_width = stored_keys.shape
    bf16, f32 = jnp.bfloat16, jnp.float32
    smem, vmem, hbm = pltpu.SMEM, pltpu.VMEM, pltpu.HBM

    def permute(v, flip=0, shift=0, core_shift=0):
        pairs = []
        for a in range(n):
            to = (a // QUAD + shift) % far * QUAD + (a % QUAD ^ flip)
            for c in range(tp_size):
                pairs.append((a * tp_size + c, to * tp_size + (c + core_shift) % tp_size))
        return lax.ppermute(v, ("ctx", "tp"), pairs)

    down, up = adapter_down[0].T, adapter_up[0]
    packed = (rank // 2 + rank // 4, wide)
    pair, hidden_pair = ((2, *packed), bf16), ((2, tokens, wide), bf16)
    sems = [pltpu.SemaphoreType.DMA((14,))]

    sx, sz, hz = call(
        first_kernel, [pair, pair, hidden_pair], specs(hbm, 3), specs(vmem, 3), sems
    )(down, up, hidden)
    gz = permute(hz, 2)
    rx = permute(sx, 1)
    rz = permute(sz, 2)
    ox, oz, hh = call(
        own_kernel, [pair, pair, hidden_pair], specs(hbm, 3), specs(vmem, 3), sems
    )(down, up, hidden)

    hx, hf = call(hidden_kernel, [hidden_pair, hidden_pair], specs(vmem, 2), specs(vmem, 2))(hh, gz)
    hg = permute(hx, 1)
    hid = [hf] + [permute(hf, 0, s) for s in range(1, far)]
    hid += [hg] + [permute(hg, 0, s) for s in range(1, far)]

    s2z, s2x = call(
        second_kernel,
        [(packed, bf16), (packed, bf16)],
        specs(smem, 1) + specs(vmem, 4),
        specs(vmem, 2),
    )(adapter_owner, ox, oz, rx, rz)
    r2z = permute(s2z, 2)
    r2x = permute(s2x, 1)
    parts = (adapter_owner, ox, oz, rx, rz, r2z, r2x)

    (mine,) = call(
        up_kernel, [((rank, quarter), bf16)], specs(smem, 1) + specs(vmem, 6), specs(vmem, 1)
    )(*parts)
    quarters = mine
    for s in range(1, far):
        came = permute(mine, 0, s)
        quarters = jnp.where((quad - owner_quad) % far == s, came, quarters)
    up_z = permute(quarters, 2)
    up_x = permute(quarters, 1)
    up_zx = permute(quarters, 3)

    partial_shape = ((2, far, tokens, rank), f32)
    keep, send = call(
        functools.partial(lowrank_kernel, far),
        [partial_shape, partial_shape],
        specs(smem, 1) + specs(vmem, 6 + 2 * far),
        specs(vmem, 2),
        [pltpu.VMEM((rank, wide), bf16), pltpu.VMEM((n * tokens, wide), bf16)],
    )(*parts, *hid)
    total = keep
    for c in range(tp_size):
        total = total + permute(send, 1, 0, c)
        if c:
            total = total + permute(keep, 0, 0, c)
    total = total[0] + permute(total[1], 2)
    low = [total[0]] + [permute(total[s], 0, -s) for s in range(1, far)]

    positions = turn_start[0] + myself * tokens + jnp.arange(tokens, dtype=jnp.int32)
    lanes = jnp.arange(HEAD_SIZE, dtype=jnp.int32)
    place_in_half = (lanes % (HEAD_SIZE // 2)).astype(f32)
    inverse = jnp.exp(place_in_half * (-2.0 * math.log(500000.0) / HEAD_SIZE))
    angles = positions.astype(f32)[:, None] * inverse[None, :]
    cosine = jnp.cos(angles)
    sine = jnp.sin(angles) * jnp.where(lanes < HEAD_SIZE // 2, -1.0, 1.0)[None, :]
    kv_rows = 2 * (slots + tokens)
    (kv,) = call(pack_kernel, [((kv_rows, kv_width), bf16)], specs(vmem, 6), specs(vmem, 1))(
        cosine, sine, stored_keys, stored_values, unrotated_turn_keys, incoming_values
    )
    kv = jnp.stack([kv] + [permute(kv, 0, s) for s in range(1, far)])
    kv_z = permute(kv, 2)
    kv_x = permute(jnp.concatenate([kv, kv_z]), 1)

    (out,) = call(
        functools.partial(attend_kernel, far, slots),
        [(q_base.shape, bf16)],
        specs(smem, 2) + specs(vmem, far + QUAD + 6),
        specs(vmem, 1),
        [
            pltpu.VMEM((QUAD, tokens, quarter), f32),
            pltpu.VMEM((kv_width // HEAD_SIZE, columns // kv_width * tokens, HEAD_SIZE), bf16),
            pltpu.VMEM((n * kv_rows // 2, kv_width), bf16),
            pltpu.VMEM((n * kv_rows // 2, kv_width), bf16),
            pltpu.VMEM((tokens, rank), f32),
        ],
        room=16 * 2**20,
        keep=False,
    )(adapter_owner, shard_lengths, *low, quarters, up_z, up_x, up_zx, kv, kv_z, kv_x, cosine, sine, q_base)
    return out


def fits_quads(mesh, hidden, q_base, adapter_down, stored_keys):
    n, tp_size = mesh.shape["ctx"], mesh.shape["tp"]
    if n % QUAD or n == QUAD:
        return False
    wide_whole = hidden.shape[1] % (tp_size * QUAD * LANES) == 0
    quarter_whole = q_base.shape[1] % (QUAD * LANES) == 0
    packs = adapter_down.shape[2] % 64 == 0 and hidden.shape[1] // tp_size == 2 * q_base.shape[1]
    rows = n * (stored_keys.shape[0] + q_base.shape[0])
    kv_width = stored_keys.shape[1]
    queries = q_base.shape[1] // kv_width * q_base.shape[0]
    room = rows * (8 * kv_width + 12 * queries)
    return wide_whole and quarter_whole and packs and room < 16 * 2**20


def solution(mesh):
    def shards(*args):
        hidden, q_base, adapter_down, stored_keys = args[0], args[1], args[2], args[7]
        if fits_quads(mesh, hidden, q_base, adapter_down, stored_keys):
            return shards_quads(*args)
        return shards_any(*args)

    return jax.shard_map(
        shards,
        mesh=mesh,
        in_specs=(
            P(("group", "ctx"), None),
            P(("group", "ctx"), "tp"),
            P(("group", "ctx"), None, None),
            P(("group", "ctx"), None, "tp"),
            P("group"),
            P("group"),
            P("group"),
            P(("group", "ctx"), "tp"),
            P(("group", "ctx"), "tp"),
            P(("group", "ctx"), "tp"),
            P(("group", "ctx"), "tp"),
        ),
        out_specs=P(("group", "ctx"), "tp"),
        check_vma=False,
    )
```
